32 devices in a mesh: dp: 8 (over y, x, core), tensor: 4 (over z).
Axes of the slice: x: 2, y: 2, z: 4, core: 2. Of those that a mesh axis runs over, the one named last changes fastest.
Arguments:
- norm_input: bfloat16 [16384, 8192], P(('dp', 'tensor')), may hold values from -6 to 6
- key_grad: bfloat16 [16384, 512], P(('dp', 'tensor')), may hold values from -100 to 100
- positions: int32 [16384], P(('dp', 'tensor')), may hold values from 0 to 8191
- norm_gain: bfloat16 [8192], replicated, may hold values from 0.25 to 1.75
- key_weight: bfloat16 [512, 8192], P('dp', 'tensor'), may hold values from -0.0625 to 0.0625
- first_moment: float32 [512, 8192], P('dp', 'tensor'), may hold values from -6 to 6
- second_moment: float32 [512, 8192], P('dp', 'tensor'), may hold values from 0.1 to 4
Outputs:
- input_grad: bfloat16 [16384, 8192], P(('dp', 'tensor'))
- new_weight: bfloat16 [512, 8192], P(None, 'tensor')
- new_first: float32 [512, 8192], P('dp', 'tensor')
- new_second: float32 [512, 8192], P('dp', 'tensor')
The draws below stay inside these ranges and needn't reach their ends.
All inputs are finite; a program needn't handle non-finite values.
Results may differ from the reference program's by a relative error of at most 0.01.
Values may be sent and summed in bfloat16 or wider, within the bound.
A program may use at most 128 MiB of HBM per device.

```python
import math
import jax
import jax.numpy as jnp
from jax import lax

D = 8192
KV_HEADS = 4
HEAD = 128
TOK_DEV = 2048
KV = 512
TOKENS = 16384
N_DP = 8


def draw_key_grad(key, part):
    key_base = jax.random.fold_in(key, 11)
    key_column = jax.random.fold_in(key, 12)
    column_rise = jnp.arange(KV, dtype=jnp.float32) / KV
    column_jitter = jax.random.uniform(key_column, (KV,), jnp.float32, 0.0, 0.3)
    column_scale = 0.3 * 10.0 ** (column_rise + column_jitter)
    values = jax.random.truncated_normal(key_base, -4.0, 4.0, (TOKENS, KV), jnp.float32) * column_scale[None, :]
    return values.astype(jnp.bfloat16)


def set_ends(values, rng, smallest, top_value):
    longest = values.shape.index(max(values.shape))
    spots = []
    for shift in (0, 1):
        where = [jax.random.randint(jax.random.fold_in(rng, axis), (), 0, length) for axis, length in enumerate(values.shape)]
        where[longest] = (where[longest] + shift) % values.shape[longest]
        spots.append(tuple(where))
    return values.at[spots[0]].set(smallest).at[spots[1]].set(top_value)


def shard_levels(stream_key, extent, split, least, top_value):
    gain = 1.0
    for dim, blocks in split:
        steps = jax.random.uniform(jax.random.fold_in(jax.random.fold_in(stream_key, 6), dim), (blocks,), jnp.float32, least / len(split), top_value / len(split))
        gain = gain * jnp.repeat(jnp.exp(steps), extent[dim] // blocks).reshape((-1,) + (1,) * (len(extent) - 1 - dim))
    return gain


def centred(stream_key, extent, scale, reach, split=(), kind=jnp.bfloat16):
    drawn = scale * jax.random.normal(stream_key, extent, jnp.float32)
    if split:
        drawn = drawn * shard_levels(stream_key, extent, split, -0.22, 0.18)
    return jnp.clip(drawn, -reach, reach).astype(kind)


def setup_inputs(seed: int = 0) -> dict:
    splits = jax.random.split(jax.random.key(seed), 8)
    norm_input = centred(splits[0], (TOKENS, D), 1.0, 6.0, ((0, 32),))
    key_grad = draw_key_grad(jax.random.fold_in(splits[7], 71), 0)
    positions = set_ends(jax.random.randint(splits[2], (TOKENS,), 0, 8192), jax.random.fold_in(splits[2], 1), 0, 8191).astype(jnp.int32)
    norm_gain = jnp.clip(1.0 + 0.15 * jax.random.normal(splits[3], (D,), jnp.float32), 0.25, 1.75).astype(jnp.bfloat16)
    key_weight = centred(splits[4], (KV, D), D ** -0.5, 0.0625, ((0, 8), (1, 4)))
    first_moment = centred(splits[5], (KV, D), 1.0, 6.0, ((0, 8), (1, 4)), jnp.float32)
    second_moment = jnp.clip(jnp.exp(math.log(4.0) - 3.6888794 * jax.random.uniform(splits[6], (KV, D), jnp.float32) ** shard_levels(splits[6], (KV, D), ((0, 8), (1, 4)), -0.2, 0.2)), 0.1, 4.0)
    return {"norm_input": norm_input, "key_grad": key_grad, "positions": positions, "norm_gain": norm_gain, "key_weight": key_weight, "first_moment": first_moment, "second_moment": second_moment}


eps_norm = 1e-05
beta_one = 0.9
beta_two = 0.95
learn_rate = 0.0003
decay_rate = 0.1
eps_adam = 1e-08

def unrotate(incoming, positions):
    row_count = incoming.shape[0]
    half_width = HEAD // 2
    frequency = 500000.0 ** (-(2.0 * jnp.arange(half_width, dtype=jnp.float32)) / HEAD)
    angles = positions.astype(jnp.float32)[:, None] * frequency[None, :]
    cosine = jnp.cos(angles)[:, None, :]
    sine_table = jnp.sin(angles)[:, None, :]
    pieces = incoming.astype(jnp.float32).reshape(row_count, KV_HEADS, 2, half_width)
    first_half = pieces[:, :, 0, :]
    second_half = pieces[:, :, 1, :]
    upper_part = first_half * cosine + second_half * sine_table
    lower_part = second_half * cosine - first_half * sine_table
    return jnp.stack([upper_part, lower_part], axis=2).reshape(row_count, KV).astype(jnp.bfloat16)

def reference(norm_input, key_grad, positions, norm_gain, key_weight, first_moment, second_moment):
    gain_f32 = norm_gain.astype(jnp.float32)
    key_back = unrotate(key_grad, positions)
    inputs = norm_input.reshape(N_DP, TOK_DEV, D)
    cotangents = key_back.reshape(N_DP, TOK_DEV, KV)

    def one_group(total, group):
        inputs_g, keys_g = group
        inputs_f32 = inputs_g.astype(jnp.float32)
        scale_inv = lax.rsqrt(lax.optimization_barrier(jnp.mean(inputs_f32 * inputs_f32, axis=1, keepdims=True)) + eps_norm)
        normalized = inputs_f32 * scale_inv
        normed = (normalized * gain_f32).astype(jnp.bfloat16)
        upstream = jnp.dot(keys_g, key_weight, preferred_element_type=jnp.float32)
        weighted = upstream * gain_f32
        inner = lax.optimization_barrier(jnp.mean(weighted * normalized, axis=1, keepdims=True))
        group_grad = (scale_inv * (weighted - normalized * inner)).astype(jnp.bfloat16)
        partial_sum = lax.dot_general(keys_g, normed, (((0,), (0,)), ((), ())), preferred_element_type=jnp.float32)
        rounded = lax.optimization_barrier(partial_sum.astype(jnp.bfloat16))
        return (total + rounded.astype(jnp.float32), group_grad)
    weight_grad, grads = lax.scan(one_group, jnp.zeros((KV, D), jnp.float32), (inputs, cotangents))
    input_grad = grads.reshape(TOKENS, D)
    clip_limit = math.sqrt(KV * D)
    grad_size = jnp.sqrt(jnp.sum(weight_grad * weight_grad))
    clip_factor = jnp.minimum(1.0, clip_limit / (grad_size + 1e-06))
    clipped = weight_grad * clip_factor
    new_first = beta_one * first_moment + (1.0 - beta_one) * clipped
    new_second = beta_two * second_moment + (1.0 - beta_two) * clipped * clipped
    weight_f32 = key_weight.astype(jnp.float32)
    new_weight = (weight_f32 * (1.0 - learn_rate * decay_rate) - learn_rate * new_first / (jnp.sqrt(new_second) + eps_adam)).astype(jnp.bfloat16)
    return (input_grad, new_weight, new_first, new_second)
```

```python
import functools
import math

import jax
import jax.numpy as jnp
from jax import lax
from jax.experimental import pallas as pl
from jax.experimental.pallas import tpu as pltpu
from jax.sharding import PartitionSpec as P

KV_HEADS = 4
HEAD = 128


eps_norm = 1e-05
beta_one = 0.9
beta_two = 0.95
learn_rate = 0.0003
decay_rate = 0.1
eps_adam = 1e-08


def unrotate(incoming, positions):
    row_count = incoming.shape[0]
    half_width = HEAD // 2
    frequency = 500000.0 ** (-(2.0 * jnp.arange(half_width, dtype=jnp.float32)) / HEAD)
    angles = positions.astype(jnp.float32)[:, None] * frequency[None, :]
    cosine = jnp.cos(angles)[:, None, :]
    sine_table = jnp.sin(angles)[:, None, :]
    pieces = incoming.astype(jnp.float32).reshape(row_count, KV_HEADS, 2, half_width)
    first_half = pieces[:, :, 0, :]
    second_half = pieces[:, :, 1, :]
    upper_part = first_half * cosine + second_half * sine_table
    lower_part = second_half * cosine - first_half * sine_table
    return (
        jnp.stack([upper_part, lower_part], axis=2)
        .reshape(row_count, KV_HEADS * HEAD)
        .astype(jnp.bfloat16)
    )


MESH = pl.DeviceIdType.MESH
F32 = jnp.float32
BF16 = jnp.bfloat16


def kernel(
    ndp, nt, x_hbm, kb, kbt, gain, w, m1, m2,
    ig_hbm, nw_hbm, nf, ns,
    x, normed, wf, wg, rcore, rq, zs, rz, gsum, up, sinv, cross, nwb, nsend, nrecv,
    lsem, xsem, osem, a1s, a1r, a2s, a2r, a3s, a3r, cs, cr, qs, qr, zsd, zr, nss, nsr, ws, wr,
):
    nq = ndp // 2
    rows, cols = w.shape
    half = nq * rows
    tokens, width = x.shape
    tile = min(128, tokens)
    ntile = tokens // tile
    cc = min(512, cols)
    dp = lax.axis_index("dp")
    t = lax.axis_index("tensor")
    c = dp % 2
    q = dp // 2
    mate = q * 2 + (1 - c)
    sends = []

    def remote(src, dst, ssem, rsem, dev):
        copy = pltpu.make_async_remote_copy(
            src_ref=src, dst_ref=dst, send_sem=ssem, recv_sem=rsem, device_id=dev, device_id_type=MESH
        )
        copy.start()
        sends.append(copy)
        return copy

    def peer_q(k):
        return ((q + k) % nq) * 2 + c

    def peer_t(i):
        return (t + 1 + i) % nt

    x_in = []
    for k in range(ntile):
        piece = pl.ds(k * tile, tile)
        copy = pltpu.make_async_copy(x_hbm.at[piece], x.at[piece], xsem.at[k])
        copy.start()
        x_in.append(copy)
    my_rows = pl.ds(pl.multiple_of((c * nq + q) * rows, rows), rows)
    own = pltpu.make_async_copy(w, wf.at[t, my_rows], lsem)
    own.start()

    barrier = pltpu.get_barrier_semaphore()
    pl.semaphore_signal(barrier, inc=1, device_id=(mate, t), device_id_type=MESH)
    for k in range(1, nq):
        pl.semaphore_signal(barrier, inc=1, device_id=(peer_q(k), t), device_id_type=MESH)
    for i in range(nt - 1):
        pl.semaphore_signal(barrier, inc=1, device_id=(dp, peer_t(i)), device_id_type=MESH)
    pl.semaphore_wait(barrier, 1 + (nq - 1) + (nt - 1))

    a1 = [remote(w, wf.at[t, my_rows], a1s.at[i], a1r.at[i], (dp, peer_t(i))) for i in range(nt - 1)]

    for k in range(ntile):
        x_in[k].wait()

        @pl.loop(0, tile // 16)
        def _(g):
            r = pl.ds(pl.multiple_of(k * tile + g * 16, 16), 16)
            v = x[r, :].astype(F32)
            s = lax.rsqrt(jnp.sum(v * v, axis=1, keepdims=True) / width + eps_norm)
            sinv[r, :] = jnp.broadcast_to(s, (16, 128))
            normed[r, :] = (v * s * gain[...]).astype(BF16)

    def product(j):
        @pl.loop(0, cols // cc)
        def _(h):
            off = pl.multiple_of(h * cc, cc)
            col = pl.ds(pl.multiple_of(j * cols + h * cc, cc), cc)
            wg[j, :, pl.ds(off, cc)] = jnp.dot(
                kbt[...], normed[:, col], preferred_element_type=F32
            ).astype(BF16)

    mine = pl.multiple_of(c * half, half)
    theirs = pl.multiple_of((1 - c) * half, half)
    core_copies = []
    q_copies = []

    def pair_sum(i):
        j = peer_t(i)
        core_copies[i].wait_recv()

        @pl.loop(0, half // 16)
        def _(g):
            r = pl.ds(pl.multiple_of(mine + g * 16, 16), 16)
            a = wg[j, r, :].astype(F32) + rcore[j, pl.ds(pl.multiple_of(g * 16, 16), 16), :].astype(F32)
            wg[j, r, :] = a.astype(BF16)

        batch = []
        for k in range(1, nq):
            r = pl.ds(pl.multiple_of(mine + ((q + k) % nq) * rows, rows), rows)
            n = i * (nq - 1) + k - 1
            batch.append(remote(wg.at[j, r], rq.at[i, k - 1], qs.at[n], qr.at[n], (peer_q(k), t)))
        q_copies.append(batch)

    for i in range(nt):
        j = peer_t(i)
        product(j)
        core_copies.append(
            remote(wg.at[j, pl.ds(theirs, half)], rcore.at[j], cs.at[i], cr.at[i], (mate, t))
        )
        if i > 0:
            pair_sum(i - 1)
    pair_sum(nt - 1)

    own.wait()
    a2 = []
    for i in range(nt):
        if i > 0:
            a1[i - 1].wait_recv()
        j = (t + nt - i) % nt
        batch = []
        for k in range(1, nq):
            n = i * (nq - 1) + k - 1
            batch.append(
                remote(wf.at[j, my_rows], wf.at[j, my_rows], a2s.at[n], a2r.at[n], (peer_q(k), t))
            )
        a2.append(batch)

    z_copies = []
    for i in range(nt):
        j = peer_t(i)
        for copy in q_copies[i]:
            copy.wait_recv()

        @pl.loop(0, rows // 16)
        def _(g):
            r = pl.ds(pl.multiple_of(g * 16, 16), 16)
            a = wg[j, pl.ds(pl.multiple_of(mine + q * rows + g * 16, 16), 16), :].astype(F32)
            for k in range(nq - 1):
                a = a + rq[i, k, r, :].astype(F32)
            if i < nt - 1:
                zs[i, r, :] = a.astype(BF16)
            else:
                gsum[r, :] = a

        if i < nt - 1:
            z_copies.append(remote(zs.at[i], rz.at[i], zsd.at[i], zr.at[i], (dp, j)))
    for copy in z_copies:
        copy.wait_recv()

    nsend[0] = jnp.zeros((8, 128), F32)

    @pl.loop(0, rows // 16)
    def _(g):
        r = pl.ds(pl.multiple_of(g * 16, 16), 16)
        a = gsum[r, :]
        for i in range(nt - 1):
            a = a + rz[i, r, :].astype(F32)
        gsum[r, :] = a
        a = a * a
        a = a[:8] + a[8:]
        total = a[:, :128]
        for k in range(1, cols // 128):
            total = total + a[:, k * 128 : (k + 1) * 128]
        nsend[0] += total

    copy = remote(nsend.at[0], nrecv.at[0], nss.at[0], nsr.at[0], (mate, t))
    copy.wait_recv()
    nsend[1] = nsend[0] + nrecv[0]
    batch = [
        remote(nsend.at[1], nrecv.at[k], nss.at[k], nsr.at[k], (peer_q(k), t)) for k in range(1, nq)
    ]
    v = nsend[1]
    for k, copy in enumerate(batch):
        copy.wait_recv()
        v = v + nrecv[k + 1]
    nsend[2] = v
    batch = [
        remote(nsend.at[2], nrecv.at[nq + i], nss.at[nq + i], nsr.at[nq + i], (dp, peer_t(i)))
        for i in range(nt - 1)
    ]
    for i, copy in enumerate(batch):
        copy.wait_recv()
        v = v + nrecv[nq + i]
    total_square = jnp.sum(jnp.sum(v, axis=1, keepdims=True), axis=0, keepdims=True)
    limit = math.sqrt(kbt.shape[0] * width)
    clip = jnp.minimum(1.0, limit / (jnp.sqrt(total_square) + 1e-06))
    slot = pl.multiple_of(c * rows, rows)

    @pl.loop(0, rows // 16)
    def _(g):
        r = pl.ds(pl.multiple_of(g * 16, 16), 16)
        clipped = gsum[r, :] * clip
        first = beta_one * m1[r, :] + (1.0 - beta_one) * clipped
        second = beta_two * m2[r, :] + (1.0 - beta_two) * clipped * clipped
        nf[r, :] = first
        ns[r, :] = second
        nwb[q, pl.ds(pl.multiple_of(slot + g * 16, 16), 16), :] = (
            w[r, :].astype(F32) * (1.0 - learn_rate * decay_rate)
            - learn_rate * first / (jnp.sqrt(second) + eps_adam)
        ).astype(BF16)

    part = nwb.at[q, pl.ds(slot, rows)]
    w_copies = [remote(part, part, ws.at[k], wr.at[k], (peer_q(k), t)) for k in range(1, nq)]

    a3 = []
    for i in range(nt):
        for copy in a2[i]:
            copy.wait_recv()
        j = (t + nt - i) % nt
        part = wf.at[j, pl.ds(mine, half)]
        a3.append(remote(part, part, a3s.at[i], a3r.at[i], (mate, t)))
    for copy in a3:
        copy.wait_recv()

    per = cols // cc
    outs = []
    for k in range(ntile):
        piece = pl.ds(k * tile, tile)
        cross[...] = jnp.zeros_like(cross)

        @pl.loop(0, width // cc)
        def _(h):
            col = pl.ds(pl.multiple_of(h * cc, cc), cc)
            u = jnp.dot(
                kb[piece, :],
                wf[h // per, :, pl.ds(pl.multiple_of((h % per) * cc, cc), cc)],
                preferred_element_type=F32,
            ) * gain[:, col]
            up[:, col] = u
            p = u * x[piece, col].astype(F32)
            total = p[:, :128]
            for b in range(1, cc // 128):
                total = total + p[:, b * 128 : (b + 1) * 128]
            cross[...] += total

        @pl.loop(0, tile // 16)
        def _(g):
            l = pl.ds(pl.multiple_of(g * 16, 16), 16)
            r = pl.ds(pl.multiple_of(k * tile + g * 16, 16), 16)
            s = sinv[r, :1]
            inner = s * (jnp.sum(cross[l, :], axis=1, keepdims=True) / width)
            normed[r, :] = (s * (up[l, :] - x[r, :].astype(F32) * s * inner)).astype(BF16)

        copy = pltpu.make_async_copy(normed.at[piece], ig_hbm.at[piece], osem.at[k])
        copy.start()
        outs.append(copy)

    for copy in w_copies:
        copy.wait_recv()
    part = nwb.at[:, pl.ds(slot, rows)]
    last = remote(part, part, ws.at[0], wr.at[0], (mate, t))
    last.wait_recv()
    copy = pltpu.make_async_copy(nwb, nw_hbm, lsem)
    copy.start()
    for copy_out in outs:
        copy_out.wait()
    for sent in sends:
        sent.wait_send()
    copy.wait()


def body(ndp, nt, norm_input, key_grad, positions, norm_gain, key_weight, first_moment, second_moment):
    rows, cols = key_weight.shape
    tokens, width = norm_input.shape
    nq = ndp // 2
    features = ndp * rows
    back = unrotate(key_grad, positions)
    back = back.reshape(tokens, nq, 2, rows).transpose(0, 2, 1, 3).reshape(tokens, features)
    tile = min(128, tokens)
    ntile = tokens // tile
    any_spec = pl.BlockSpec(memory_space=pl.ANY)
    vmem = pl.BlockSpec(memory_space=pltpu.VMEM)
    dma = pltpu.SemaphoreType.DMA
    scratch = [
        pltpu.VMEM((tokens, width), BF16),
        pltpu.VMEM((tokens, width), BF16),
        pltpu.VMEM((nt, features, cols), BF16),
        pltpu.VMEM((nt, features, cols), BF16),
        pltpu.VMEM((nt, nq * rows, cols), BF16),
        pltpu.VMEM((nt, nq - 1, rows, cols), BF16),
        pltpu.VMEM((nt - 1, rows, cols), BF16),
        pltpu.VMEM((nt - 1, rows, cols), BF16),
        pltpu.VMEM((rows, cols), F32),
        pltpu.VMEM((tile, width), F32),
        pltpu.VMEM((tokens, 128), F32),
        pltpu.VMEM((tile, 128), F32),
        pltpu.VMEM((nq, 2 * rows, cols), BF16),
        pltpu.VMEM((3, 8, 128), F32),
        pltpu.VMEM((nq + nt - 1, 8, 128), F32),
        dma, dma((ntile,)), dma((ntile,)),
        dma((nt - 1,)), dma((nt - 1,)),
        dma((nt * (nq - 1),)), dma((nt * (nq - 1),)),
        dma((nt,)), dma((nt,)),
        dma((nt,)), dma((nt,)),
        dma((nt * (nq - 1),)), dma((nt * (nq - 1),)),
        dma((nt - 1,)), dma((nt - 1,)),
        dma((nq + nt - 1,)), dma((nq + nt - 1,)),
        dma((nq,)), dma((nq,)),
    ]
    input_grad, new_weight, new_first, new_second = pl.pallas_call(
        functools.partial(kernel, ndp, nt),
        out_shape=(
            jax.ShapeDtypeStruct((tokens, width), BF16),
            jax.ShapeDtypeStruct((nq, 2 * rows, cols), BF16),
            jax.ShapeDtypeStruct((rows, cols), F32),
            jax.ShapeDtypeStruct((rows, cols), F32),
        ),
        in_specs=[any_spec] + [vmem] * 6,
        out_specs=(any_spec, any_spec, vmem, vmem),
        scratch_shapes=scratch,
        compiler_params=pltpu.CompilerParams(
            collective_id=0, has_side_effects=True, vmem_limit_bytes=62 * 2**20
        ),
    )(
        norm_input, back, back.T, norm_gain.astype(F32)[None, :], key_weight, first_moment, second_moment,
    )
    return (input_grad, new_weight.reshape(features, cols), new_first, new_second)


def solution(mesh):
    in_specs = (
        P(("dp", "tensor"), None),
        P(("dp", "tensor"), None),
        P(("dp", "tensor")),
        P(),
        P("dp", "tensor"),
        P("dp", "tensor"),
        P("dp", "tensor"),
    )
    out_specs = (P(("dp", "tensor"), None), P(None, "tensor"), P("dp", "tensor"), P("dp", "tensor"))
    return jax.shard_map(
        functools.partial(body, mesh.shape["dp"], mesh.shape["tensor"]),
        mesh=mesh, in_specs=in_specs, out_specs=out_specs, check_vma=False,
    )
```

```python
import functools
import math

import jax
import jax.numpy as jnp
from jax import lax
from jax.experimental import pallas as pl
from jax.experimental.pallas import tpu as pltpu
from jax.sharding import PartitionSpec as P

KV_HEADS = 4
HEAD = 128


eps_norm = 1e-05
beta_one = 0.9
beta_two = 0.95
learn_rate = 0.0003
decay_rate = 0.1
eps_adam = 1e-08


def unrotate(incoming, positions):
    row_count = incoming.shape[0]
    half_width = HEAD // 2
    frequency = 500000.0 ** (-(2.0 * jnp.arange(half_width, dtype=jnp.float32)) / HEAD)
    angles = positions.astype(jnp.float32)[:, None] * frequency[None, :]
    cosine = jnp.cos(angles)[:, None, :]
    sine_table = jnp.sin(angles)[:, None, :]
    pieces = incoming.astype(jnp.float32).reshape(row_count, KV_HEADS, 2, half_width)
    first_half = pieces[:, :, 0, :]
    second_half = pieces[:, :, 1, :]
    upper_part = first_half * cosine + second_half * sine_table
    lower_part = second_half * cosine - first_half * sine_table
    return (
        jnp.stack([upper_part, lower_part], axis=2)
        .reshape(row_count, KV_HEADS * HEAD)
        .astype(jnp.bfloat16)
    )


MESH = pl.DeviceIdType.MESH
F32 = jnp.float32
BF16 = jnp.bfloat16


def kernel(
    ndp, nt, nqx, x_hbm, kb, kbt, gain, w, m1, m2,
    ig_hbm, nw_hbm, nf, ns,
    x, normed, wf, wg, rcore, r1a, r1b, r2a, r2b, zs, rz, gsum, sinv, cross, nwb, nsend, nrecv,
    lsem, xsem, osem, a1s, a1r, a2s, a2r, a3s, a3r, b3s, b3r, cs, cr, qs, qr, q2s, q2r,
    zsd, zr, nss, nsr, ws, wr, vs, vr,
):
    nq = ndp // 2
    nqy = nq // nqx
    rows, cols = w.shape
    half = nq * rows
    tokens, width = x.shape
    tile = min(128, tokens)
    ntile = tokens // tile
    cc = min(512, cols)
    hc = cols // 2
    ha = pl.ds(0, hc)
    hb = pl.ds(hc, hc)
    dp = lax.axis_index("dp")
    t = lax.axis_index("tensor")
    c = dp % 2
    q = dp // 2
    qy = q // nqx
    qx = q % nqx
    mate = q * 2 + (1 - c)
    mine = pl.multiple_of(c * half, half)
    theirs = pl.multiple_of((1 - c) * half, half)
    sends = []

    def remote(src, dst, ssem, rsem, dev):
        copy = pltpu.make_async_remote_copy(
            src_ref=src, dst_ref=dst, send_sem=ssem, recv_sem=rsem, device_id=dev, device_id_type=MESH
        )
        copy.start()
        sends.append(copy)
        return copy

    def pos_x(k):
        return (qx + k) % nqx

    def pos_y(k):
        return (qy + k) % nqy

    def dev_x(k):
        return ((qy * nqx + pos_x(k)) * 2 + c, t)

    def dev_y(k):
        return ((pos_y(k) * nqx + qx) * 2 + c, t)

    def slot(yy, xx):
        return pl.ds(pl.multiple_of(mine + (yy * nqx + xx) * rows, rows), rows)

    def peer_t(i):
        return (t + 1 + i) % nt

    x_in = []
    for k in range(ntile):
        piece = pl.ds(k * tile, tile)
        copy = pltpu.make_async_copy(x_hbm.at[piece], x.at[piece], xsem.at[k])
        copy.start()
        x_in.append(copy)
    my_rows = slot(qy, qx)
    own = pltpu.make_async_copy(w, wf.at[t, my_rows], lsem)
    own.start()

    barrier = pltpu.get_barrier_semaphore()
    pl.semaphore_signal(barrier, inc=1, device_id=(mate, t), device_id_type=MESH)
    for k in range(1, nqx):
        pl.semaphore_signal(barrier, inc=1, device_id=dev_x(k), device_id_type=MESH)
    for k in range(1, nqy):
        pl.semaphore_signal(barrier, inc=1, device_id=dev_y(k), device_id_type=MESH)
    for i in range(nt - 1):
        pl.semaphore_signal(barrier, inc=1, device_id=(dp, peer_t(i)), device_id_type=MESH)
    pl.semaphore_wait(barrier, 1 + (nqx - 1) + (nqy - 1) + (nt - 1))

    a1 = [remote(w, wf.at[t, my_rows], a1s.at[i], a1r.at[i], (dp, peer_t(i))) for i in range(nt - 1)]
    na = nqx + nqy - 2
    first_hop = {}
    second_hop = {}

    def block(i):
        return (t + nt - i) % nt

    def gather_first(i):
        j = block(i)
        if i > 0:
            a1[i - 1].wait_recv()
        src = w if i == 0 else wf.at[j, my_rows]
        batch = []
        for k in range(1, nqx):
            n = i * na + k - 1
            batch.append(
                remote(src.at[:, ha], wf.at[j, my_rows, ha], a2s.at[n], a2r.at[n], dev_x(k))
            )
        for k in range(1, nqy):
            n = i * na + nqx - 1 + k - 1
            batch.append(
                remote(src.at[:, hb], wf.at[j, my_rows, hb], a2s.at[n], a2r.at[n], dev_y(k))
            )
        first_hop[i] = batch

    nb = (nqx - 1) * nqy + (nqy - 1) * nqx

    def gather_second(i):
        j = block(i)
        for copy in first_hop[i]:
            copy.wait_recv()
        batch = []
        n = i * nb
        for k in range(1, nqy):
            for xx in range(nqx):
                part = wf.at[j, slot(qy, xx), ha]
                batch.append(remote(part, part, b3s.at[n], b3r.at[n], dev_y(k)))
                n += 1
        for k in range(1, nqx):
            for yy in range(nqy):
                part = wf.at[j, slot(yy, qx), hb]
                batch.append(remote(part, part, b3s.at[n], b3r.at[n], dev_x(k)))
                n += 1
        second_hop[i] = batch

    gather_first(0)
    cross[...] = jnp.zeros_like(cross)

    for k in range(ntile):
        x_in[k].wait()

        @pl.loop(0, tile // 16)
        def _(g):
            r = pl.ds(pl.multiple_of(k * tile + g * 16, 16), 16)
            v = x[r, :].astype(F32)
            s = lax.rsqrt(jnp.sum(v * v, axis=1, keepdims=True) / width + eps_norm)
            sinv[r, :] = jnp.broadcast_to(s, (16, 128))
            normed[r, :] = (v * s * gain[...]).astype(BF16)

    def product(j):
        @pl.loop(0, cols // cc)
        def _(h):
            off = pl.multiple_of(h * cc, cc)
            col = pl.ds(pl.multiple_of(j * cols + h * cc, cc), cc)
            wg[j, :, pl.ds(off, cc)] = jnp.dot(
                kbt[...], normed[:, col], preferred_element_type=F32
            ).astype(BF16)

    core_copies = []
    q_copies = []
    q2_copies = []

    def pair_sum(i):
        j = peer_t(i)
        core_copies[i].wait_recv()

        @pl.loop(0, half // 16)
        def _(g):
            r = pl.ds(pl.multiple_of(mine + g * 16, 16), 16)
            a = wg[j, r, :].astype(F32) + rcore[j, pl.ds(pl.multiple_of(g * 16, 16), 16), :].astype(F32)
            wg[j, r, :] = a.astype(BF16)

        batch = []
        n = i * nb
        for k in range(1, nqx):
            for yy in range(nqy):
                src = wg.at[j, slot(yy, pos_x(k)), ha]
                batch.append(
                    remote(src, r1a.at[i, (k - 1) * nqy + yy], qs.at[n], qr.at[n], dev_x(k))
                )
                n += 1
        for k in range(1, nqy):
            for xx in range(nqx):
                src = wg.at[j, slot(pos_y(k), xx), hb]
                batch.append(
                    remote(src, r1b.at[i, (k - 1) * nqx + xx], qs.at[n], qr.at[n], dev_y(k))
                )
                n += 1
        q_copies.append(batch)

    for i in range(nt):
        j = peer_t(i)
        product(j)
        core_copies.append(
            remote(wg.at[j, pl.ds(theirs, half)], rcore.at[j], cs.at[i], cr.at[i], (mate, t))
        )
        if i > 0:
            pair_sum(i - 1)
    pair_sum(nt - 1)
    own.wait()

    def middle(i):
        j = peer_t(i)
        for copy in q_copies[i]:
            copy.wait_recv()

        @pl.loop(0, rows // 16)
        def _(g):
            l = pl.ds(pl.multiple_of(g * 16, 16), 16)
            for yy in range(nqy):
                r = pl.ds(pl.multiple_of(mine + (yy * nqx + qx) * rows + g * 16, 16), 16)
                a = wg[j, r, ha].astype(F32)
                for k in range(nqx - 1):
                    a = a + r1a[i, k * nqy + yy, l, :].astype(F32)
                wg[j, r, ha] = a.astype(BF16)
            for xx in range(nqx):
                r = pl.ds(pl.multiple_of(mine + (qy * nqx + xx) * rows + g * 16, 16), 16)
                a = wg[j, r, hb].astype(F32)
                for k in range(nqy - 1):
                    a = a + r1b[i, k * nqx + xx, l, :].astype(F32)
                wg[j, r, hb] = a.astype(BF16)

        batch = []
        n = i * na
        for k in range(1, nqy):
            batch.append(
                remote(wg.at[j, slot(pos_y(k), qx), ha], r2a.at[i, k - 1], q2s.at[n], q2r.at[n], dev_y(k))
            )
            n += 1
        for k in range(1, nqx):
            batch.append(
                remote(wg.at[j, slot(qy, pos_x(k)), hb], r2b.at[i, k - 1], q2s.at[n], q2r.at[n], dev_x(k))
            )
            n += 1
        q2_copies.append(batch)

    z_copies = []

    def final(i):
        j = peer_t(i)
        for copy in q2_copies[i]:
            copy.wait_recv()

        @pl.loop(0, rows // 16)
        def _(g):
            r = pl.ds(pl.multiple_of(g * 16, 16), 16)
            m = pl.ds(pl.multiple_of(mine + q * rows + g * 16, 16), 16)
            for part, other, count in ((ha, r2a, nqy - 1), (hb, r2b, nqx - 1)):
                a = wg[j, m, part].astype(F32)
                for k in range(count):
                    a = a + other[i, k, r, :].astype(F32)
                if i < nt - 1:
                    zs[i, r, part] = a.astype(BF16)
                else:
                    gsum[r, part] = a

        if i < nt - 1:
            z_copies.append(remote(zs.at[i], rz.at[i], zsd.at[i], zr.at[i], (dp, j)))

    gather_second(0)
    for i in range(nt):
        middle(i)
        if i > 0:
            gather_first(i)
    for i in range(nt):
        final(i)
        if i > 0:
            gather_second(i)

    a3 = {}

    def gather_third(i):
        for copy in second_hop[i]:
            copy.wait_recv()
        part = wf.at[block(i), pl.ds(mine, half)]
        a3[i] = remote(part, part, a3s.at[i], a3r.at[i], (mate, t))

    uc = min(256, cols)

    def upstream(i):
        j = block(i)
        a3[i].wait_recv()

        @pl.loop(0, cols // uc)
        def _(h):
            off = pl.ds(pl.multiple_of(h * uc, uc), uc)
            col = pl.ds(pl.multiple_of(j * cols + h * uc, uc), uc)
            u = jnp.dot(kb[...], wf[j, :, off], preferred_element_type=F32) * gain[:, col]
            normed[:, col] = u.astype(BF16)
            p = u * x[:, col].astype(F32)
            total = p[:, :128]
            for b in range(1, uc // 128):
                total = total + p[:, b * 128 : (b + 1) * 128]
            cross[...] += total

    gather_third(0)
    upstream(0)
    for copy in z_copies:
        copy.wait_recv()

    nsend[0] = jnp.zeros((8, 128), F32)

    @pl.loop(0, rows // 16)
    def _(g):
        r = pl.ds(pl.multiple_of(g * 16, 16), 16)
        a = gsum[r, :]
        for i in range(nt - 1):
            a = a + rz[i, r, :].astype(F32)
        gsum[r, :] = a
        a = a * a
        a = a[:8] + a[8:]
        total = a[:, :128]
        for k in range(1, cols // 128):
            total = total + a[:, k * 128 : (k + 1) * 128]
        nsend[0] += total

    base = 0
    v = nsend[0]
    groups = (
        [(mate, t)],
        [dev_x(k) for k in range(1, nqx)],
        [dev_y(k) for k in range(1, nqy)],
        [(dp, peer_t(i)) for i in range(nt - 1)],
    )
    for step, devs in enumerate(groups):
        if step > 0:
            nsend[step] = v
        batch = [
            remote(nsend.at[step], nrecv.at[base + n], nss.at[base + n], nsr.at[base + n], dev)
            for n, dev in enumerate(devs)
        ]
        for n, copy in enumerate(batch):
            copy.wait_recv()
            v = v + nrecv[base + n]
        base += len(devs)
    total_square = jnp.sum(jnp.sum(v, axis=1, keepdims=True), axis=0, keepdims=True)
    limit = math.sqrt(kbt.shape[0] * width)
    clip = jnp.minimum(1.0, limit / (jnp.sqrt(total_square) + 1e-06))
    nat = pl.multiple_of(c * rows, rows)

    @pl.loop(0, rows // 16)
    def _(g):
        r = pl.ds(pl.multiple_of(g * 16, 16), 16)
        clipped = gsum[r, :] * clip
        first = beta_one * m1[r, :] + (1.0 - beta_one) * clipped
        second = beta_two * m2[r, :] + (1.0 - beta_two) * clipped * clipped
        nf[r, :] = first
        ns[r, :] = second
        nwb[q, pl.ds(pl.multiple_of(nat + g * 16, 16), 16), :] = (
            w[r, :].astype(F32) * (1.0 - learn_rate * decay_rate)
            - learn_rate * first / (jnp.sqrt(second) + eps_adam)
        ).astype(BF16)

    def piece_of(yy, xx, part):
        return nwb.at[yy * nqx + xx, pl.ds(nat, rows), part]

    w_first = []
    for k in range(1, nqx):
        part = piece_of(qy, qx, ha)
        w_first.append(remote(part, part, ws.at[k - 1], wr.at[k - 1], dev_x(k)))
    for k in range(1, nqy):
        n = nqx - 1 + k - 1
        part = piece_of(qy, qx, hb)
        w_first.append(remote(part, part, ws.at[n], wr.at[n], dev_y(k)))

    for i in range(1, nt):
        gather_third(i)
        upstream(i)

    for copy in w_first:
        copy.wait_recv()
    w_second = []
    for k in range(1, nqy):
        for xx in range(nqx):
            part = piece_of(qy, xx, ha)
            n = len(w_second)
            w_second.append(remote(part, part, vs.at[n], vr.at[n], dev_y(k)))
    for k in range(1, nqx):
        for yy in range(nqy):
            part = piece_of(yy, qx, hb)
            n = len(w_second)
            w_second.append(remote(part, part, vs.at[n], vr.at[n], dev_x(k)))

    outs = []
    for k in range(ntile):
        piece = pl.ds(k * tile, tile)

        @pl.loop(0, tile // 16)
        def _(g):
            r = pl.ds(pl.multiple_of(k * tile + g * 16, 16), 16)
            s = sinv[r, :1]
            inner = s * (jnp.sum(cross[r, :], axis=1, keepdims=True) / width)
            normed[r, :] = (
                s * (normed[r, :].astype(F32) - x[r, :].astype(F32) * s * inner)
            ).astype(BF16)

        copy = pltpu.make_async_copy(normed.at[piece], ig_hbm.at[piece], osem.at[k])
        copy.start()
        outs.append(copy)

    for copy in w_second:
        copy.wait_recv()
    part = nwb.at[:, pl.ds(nat, rows)]
    last = remote(part, part, vs.at[nb], vr.at[nb], (mate, t))
    last.wait_recv()
    copy = pltpu.make_async_copy(nwb, nw_hbm, lsem)
    copy.start()
    for copy_out in outs:
        copy_out.wait()
    for sent in sends:
        sent.wait_send()
    copy.wait()


def body(ndp, nt, norm_input, key_grad, positions, norm_gain, key_weight, first_moment, second_moment):
    rows, cols = key_weight.shape
    tokens, width = norm_input.shape
    nq = ndp // 2
    features = ndp * rows
    back = unrotate(key_grad, positions)
    back = back.reshape(tokens, nq, 2, rows).transpose(0, 2, 1, 3).reshape(tokens, features)
    tile = min(128, tokens)
    ntile = tokens // tile
    any_spec = pl.BlockSpec(memory_space=pl.ANY)
    vmem = pl.BlockSpec(memory_space=pltpu.VMEM)
    dma = pltpu.SemaphoreType.DMA
    nqx = math.isqrt(nq)
    while nq % nqx:
        nqx -= 1
    nqy = nq // nqx
    hc = cols // 2
    na = nqx + nqy - 2
    nb = (nqx - 1) * nqy + (nqy - 1) * nqx
    nn = 1 + na + nt - 1
    scratch = [
        pltpu.VMEM((tokens, width), BF16),
        pltpu.VMEM((tokens, width), BF16),
        pltpu.VMEM((nt, features, cols), BF16),
        pltpu.VMEM((nt, features, cols), BF16),
        pltpu.VMEM((nt, nq * rows, cols), BF16),
        pltpu.VMEM((nt, (nqx - 1) * nqy, rows, hc), BF16),
        pltpu.VMEM((nt, (nqy - 1) * nqx, rows, hc), BF16),
        pltpu.VMEM((nt, nqy - 1, rows, hc), BF16),
        pltpu.VMEM((nt, nqx - 1, rows, hc), BF16),
        pltpu.VMEM((nt - 1, rows, cols), BF16),
        pltpu.VMEM((nt - 1, rows, cols), BF16),
        pltpu.VMEM((rows, cols), F32),
        pltpu.VMEM((tokens, 128), F32),
        pltpu.VMEM((tokens, 128), F32),
        pltpu.VMEM((nq, 2 * rows, cols), BF16),
        pltpu.VMEM((4, 8, 128), F32),
        pltpu.VMEM((nn, 8, 128), F32),
        dma, dma((ntile,)), dma((ntile,)),
    ]
    for count in (nt - 1, nt * na, nt, nt * nb, nt, nt * nb, nt * na, nt - 1, nn, na, nb + 1):
        scratch += [dma((count,)), dma((count,))]
    input_grad, new_weight, new_first, new_second = pl.pallas_call(
        functools.partial(kernel, ndp, nt, nqx),
        out_shape=(
            jax.ShapeDtypeStruct((tokens, width), BF16),
            jax.ShapeDtypeStruct((nq, 2 * rows, cols), BF16),
            jax.ShapeDtypeStruct((rows, cols), F32),
            jax.ShapeDtypeStruct((rows, cols), F32),
        ),
        in_specs=[any_spec] + [vmem] * 6,
        out_specs=(any_spec, any_spec, vmem, vmem),
        scratch_shapes=scratch,
        compiler_params=pltpu.CompilerParams(
            collective_id=0, has_side_effects=True, vmem_limit_bytes=62 * 2**20
        ),
    )(
        norm_input, back, back.T, norm_gain.astype(F32)[None, :], key_weight, first_moment, second_moment,
    )
    return (input_grad, new_weight.reshape(features, cols), new_first, new_second)


def solution(mesh):
    in_specs = (
        P(("dp", "tensor"), None),
        P(("dp", "tensor"), None),
        P(("dp", "tensor")),
        P(),
        P("dp", "tensor"),
        P("dp", "tensor"),
        P("dp", "tensor"),
    )
    out_specs = (P(("dp", "tensor"), None), P(None, "tensor"), P("dp", "tensor"), P("dp", "tensor"))
    return jax.shard_map(
        functools.partial(body, mesh.shape["dp"], mesh.shape["tensor"]),
        mesh=mesh, in_specs=in_specs, out_specs=out_specs, check_vma=False,
    )
```

```python
import functools
import math

import jax
import jax.numpy as jnp
from jax import lax
from jax.experimental import pallas as pl
from jax.experimental.pallas import tpu as pltpu
from jax.sharding import PartitionSpec as P

KV_HEADS = 4
HEAD = 128


eps_norm = 1e-05
beta_one = 0.9
beta_two = 0.95
learn_rate = 0.0003
decay_rate = 0.1
eps_adam = 1e-08


def unrotate(incoming, positions):
    row_count = incoming.shape[0]
    half_width = HEAD // 2
    frequency = 500000.0 ** (-(2.0 * jnp.arange(half_width, dtype=jnp.float32)) / HEAD)
    angles = positions.astype(jnp.float32)[:, None] * frequency[None, :]
    cosine = jnp.cos(angles)[:, None, :]
    sine_table = jnp.sin(angles)[:, None, :]
    pieces = incoming.astype(jnp.float32).reshape(row_count, KV_HEADS, 2, half_width)
    first_half = pieces[:, :, 0, :]
    second_half = pieces[:, :, 1, :]
    upper_part = first_half * cosine + second_half * sine_table
    lower_part = second_half * cosine - first_half * sine_table
    return (
        jnp.stack([upper_part, lower_part], axis=2)
        .reshape(row_count, KV_HEADS * HEAD)
        .astype(jnp.bfloat16)
    )


MESH = pl.DeviceIdType.MESH
F32 = jnp.float32
BF16 = jnp.bfloat16


def kernel(
    ndp, nt, nqx, x_hbm, kb, kbt, gain, w, m1, m2,
    ig_hbm, nw_hbm, nf, ns,
    x, normed, wf, wg, rcore, r1a, r1b, r2a, r2b, zs, rz, gsum, sinv, cross, nwb, nsend, nrecv,
    lsem, xsem, osem, a1s, a1r, a2s, a2r, a3s, a3r, b3s, b3r, cs, cr, qs, qr, q2s, q2r,
    zsd, zr, nss, nsr, ws, wr, vs, vr,
):
    nq = ndp // 2
    nqy = nq // nqx
    rows, cols = w.shape
    half = nq * rows
    tokens, width = x.shape
    tile = min(128, tokens)
    ntile = tokens // tile
    cc = min(512, cols)
    hc = cols // 2
    ha = pl.ds(0, hc)
    hb = pl.ds(hc, hc)
    dp = lax.axis_index("dp")
    t = lax.axis_index("tensor")
    c = dp % 2
    q = dp // 2
    qy = q // nqx
    qx = q % nqx
    mate = q * 2 + (1 - c)
    mine = pl.multiple_of(c * half, half)
    theirs = pl.multiple_of((1 - c) * half, half)
    sends = []

    def remote(src, dst, ssem, rsem, dev):
        copy = pltpu.make_async_remote_copy(
            src_ref=src, dst_ref=dst, send_sem=ssem, recv_sem=rsem, device_id=dev, device_id_type=MESH
        )
        copy.start()
        sends.append(copy)
        return copy

    def pos_x(k):
        return (qx + k) % nqx

    def pos_y(k):
        return (qy + k) % nqy

    def dev_x(k):
        return ((qy * nqx + pos_x(k)) * 2 + c, t)

    def dev_y(k):
        return ((pos_y(k) * nqx + qx) * 2 + c, t)

    def slot(yy, xx):
        return pl.ds(pl.multiple_of(mine + (yy * nqx + xx) * rows, rows), rows)

    def peer_t(i):
        return (t + 1 + i) % nt

    x_in = []
    for k in range(ntile):
        piece = pl.ds(k * tile, tile)
        copy = pltpu.make_async_copy(x_hbm.at[piece], x.at[piece], xsem.at[k])
        copy.start()
        x_in.append(copy)
    my_rows = slot(qy, qx)
    own = pltpu.make_async_copy(w, wf.at[t, my_rows], lsem)
    own.start()

    barrier = pltpu.get_barrier_semaphore()
    pl.semaphore_signal(barrier, inc=1, device_id=(mate, t), device_id_type=MESH)
    for k in range(1, nqx):
        pl.semaphore_signal(barrier, inc=1, device_id=dev_x(k), device_id_type=MESH)
    for k in range(1, nqy):
        pl.semaphore_signal(barrier, inc=1, device_id=dev_y(k), device_id_type=MESH)
    for i in range(nt - 1):
        pl.semaphore_signal(barrier, inc=1, device_id=(dp, peer_t(i)), device_id_type=MESH)
    pl.semaphore_wait(barrier, 1 + (nqx - 1) + (nqy - 1) + (nt - 1))

    a1 = [remote(w, wf.at[t, my_rows], a1s.at[i], a1r.at[i], (dp, peer_t(i))) for i in range(nt - 1)]
    na = nqx + nqy - 2
    first_hop = {}
    second_hop = {}

    def block(i):
        return (t + nt - i) % nt

    def gather_first(i):
        j = block(i)
        if i > 0:
            a1[i - 1].wait_recv()
        src = w if i == 0 else wf.at[j, my_rows]
        batch = []
        for k in range(1, nqx):
            n = i * na + k - 1
            batch.append(
                remote(src.at[:, ha], wf.at[j, my_rows, ha], a2s.at[n], a2r.at[n], dev_x(k))
            )
        for k in range(1, nqy):
            n = i * na + nqx - 1 + k - 1
            batch.append(
                remote(src.at[:, hb], wf.at[j, my_rows, hb], a2s.at[n], a2r.at[n], dev_y(k))
            )
        first_hop[i] = batch

    nb = (nqx - 1) * nqy + (nqy - 1) * nqx

    def gather_second(i):
        j = block(i)
        for copy in first_hop[i]:
            copy.wait_recv()
        batch = []
        n = i * nb
        for k in range(1, nqy):
            for xx in range(nqx):
                part = wf.at[j, slot(qy, xx), ha]
                batch.append(remote(part, part, b3s.at[n], b3r.at[n], dev_y(k)))
                n += 1
        for k in range(1, nqx):
            for yy in range(nqy):
                part = wf.at[j, slot(yy, qx), hb]
                batch.append(remote(part, part, b3s.at[n], b3r.at[n], dev_x(k)))
                n += 1
        second_hop[i] = batch

    gather_first(0)
    cross[...] = jnp.zeros_like(cross)

    for k in range(ntile):
        x_in[k].wait()

        @pl.loop(0, tile // 16)
        def _(g):
            r = pl.ds(pl.multiple_of(k * tile + g * 16, 16), 16)
            v = x[r, :].astype(F32)
            s = lax.rsqrt(jnp.sum(v * v, axis=1, keepdims=True) / width + eps_norm)
            sinv[r, :] = jnp.broadcast_to(s, (16, 128))
            normed[r, :] = (v * s * gain[...]).astype(BF16)

        if k == ntile // 2:
            own.wait()
            gather_second(0)
        if k == ntile - 1:
            gather_first(1)

    def product(j):
        @pl.loop(0, cols // cc)
        def _(h):
            off = pl.multiple_of(h * cc, cc)
            col = pl.ds(pl.multiple_of(j * cols + h * cc, cc), cc)
            wg[j, :, pl.ds(off, cc)] = jnp.dot(
                kbt[...], normed[:, col], preferred_element_type=F32
            ).astype(BF16)

    core_copies = []
    q_copies = []
    q2_copies = []

    def pair_sum(i):
        j = peer_t(i)
        core_copies[i].wait_recv()

        @pl.loop(0, half // 16)
        def _(g):
            r = pl.ds(pl.multiple_of(mine + g * 16, 16), 16)
            a = wg[j, r, :].astype(F32) + rcore[j, pl.ds(pl.multiple_of(g * 16, 16), 16), :].astype(F32)
            wg[j, r, :] = a.astype(BF16)

        batch = []
        n = i * nb
        for k in range(1, nqx):
            for yy in range(nqy):
                src = wg.at[j, slot(yy, pos_x(k)), ha]
                batch.append(
                    remote(src, r1a.at[i, (k - 1) * nqy + yy], qs.at[n], qr.at[n], dev_x(k))
                )
                n += 1
        for k in range(1, nqy):
            for xx in range(nqx):
                src = wg.at[j, slot(pos_y(k), xx), hb]
                batch.append(
                    remote(src, r1b.at[i, (k - 1) * nqx + xx], qs.at[n], qr.at[n], dev_y(k))
                )
                n += 1
        q_copies.append(batch)

    for i in range(nt):
        j = peer_t(i)
        product(j)
        core_copies.append(
            remote(wg.at[j, pl.ds(theirs, half)], rcore.at[j], cs.at[i], cr.at[i], (mate, t))
        )
        if i == 1:
            gather_second(1)
        if i > 0:
            pair_sum(i - 1)
    pair_sum(nt - 1)

    def middle(i):
        j = peer_t(i)
        for copy in q_copies[i]:
            copy.wait_recv()

        @pl.loop(0, rows // 16)
        def _(g):
            l = pl.ds(pl.multiple_of(g * 16, 16), 16)
            for yy in range(nqy):
                r = pl.ds(pl.multiple_of(mine + (yy * nqx + qx) * rows + g * 16, 16), 16)
                a = wg[j, r, ha].astype(F32)
                for k in range(nqx - 1):
                    a = a + r1a[i, k * nqy + yy, l, :].astype(F32)
                wg[j, r, ha] = a.astype(BF16)
            for xx in range(nqx):
                r = pl.ds(pl.multiple_of(mine + (qy * nqx + xx) * rows + g * 16, 16), 16)
                a = wg[j, r, hb].astype(F32)
                for k in range(nqy - 1):
                    a = a + r1b[i, k * nqx + xx, l, :].astype(F32)
                wg[j, r, hb] = a.astype(BF16)

        batch = []
        n = i * na
        for k in range(1, nqy):
            batch.append(
                remote(wg.at[j, slot(pos_y(k), qx), ha], r2a.at[i, k - 1], q2s.at[n], q2r.at[n], dev_y(k))
            )
            n += 1
        for k in range(1, nqx):
            batch.append(
                remote(wg.at[j, slot(qy, pos_x(k)), hb], r2b.at[i, k - 1], q2s.at[n], q2r.at[n], dev_x(k))
            )
            n += 1
        q2_copies.append(batch)

    z_copies = []

    def final(i):
        j = peer_t(i)
        for copy in q2_copies[i]:
            copy.wait_recv()

        @pl.loop(0, rows // 16)
        def _(g):
            r = pl.ds(pl.multiple_of(g * 16, 16), 16)
            m = pl.ds(pl.multiple_of(mine + q * rows + g * 16, 16), 16)
            for part, other, count in ((ha, r2a, nqy - 1), (hb, r2b, nqx - 1)):
                a = wg[j, m, part].astype(F32)
                for k in range(count):
                    a = a + other[i, k, r, :].astype(F32)
                if i < nt - 1:
                    zs[i, r, part] = a.astype(BF16)
                else:
                    gsum[r, part] = a

        if i < nt - 1:
            z_copies.append(remote(zs.at[i], rz.at[i], zsd.at[i], zr.at[i], (dp, j)))

    for i in range(nt):
        middle(i)
        if i > 1:
            gather_first(i)
    for i in range(nt):
        final(i)
        if i > 1:
            gather_second(i)

    a3 = {}

    def gather_third(i):
        for copy in second_hop[i]:
            copy.wait_recv()
        part = wf.at[block(i), pl.ds(mine, half)]
        a3[i] = remote(part, part, a3s.at[i], a3r.at[i], (mate, t))

    uc = min(256, cols)

    def upstream(i):
        j = block(i)
        a3[i].wait_recv()

        @pl.loop(0, cols // uc)
        def _(h):
            off = pl.ds(pl.multiple_of(h * uc, uc), uc)
            col = pl.ds(pl.multiple_of(j * cols + h * uc, uc), uc)
            u = jnp.dot(kb[...], wf[j, :, off], preferred_element_type=F32) * gain[:, col]
            normed[:, col] = u.astype(BF16)
            p = u * x[:, col].astype(F32)
            total = p[:, :128]
            for b in range(1, uc // 128):
                total = total + p[:, b * 128 : (b + 1) * 128]
            cross[...] += total

    for i in range(2):
        gather_third(i)
        upstream(i)
    for copy in z_copies:
        copy.wait_recv()

    nsend[0] = jnp.zeros((8, 128), F32)

    @pl.loop(0, rows // 16)
    def _(g):
        r = pl.ds(pl.multiple_of(g * 16, 16), 16)
        a = gsum[r, :]
        for i in range(nt - 1):
            a = a + rz[i, r, :].astype(F32)
        gsum[r, :] = a
        a = a * a
        a = a[:8] + a[8:]
        total = a[:, :128]
        for k in range(1, cols // 128):
            total = total + a[:, k * 128 : (k + 1) * 128]
        nsend[0] += total

    base = 0
    v = nsend[0]
    groups = (
        [(mate, t)],
        [(dp, peer_t(i)) for i in range(nt - 1)],
        [dev_x(k) for k in range(1, nqx)],
        [dev_y(k) for k in range(1, nqy)],
    )
    for step, devs in enumerate(groups):
        if step > 0:
            nsend[step] = v
        batch = [
            remote(nsend.at[step], nrecv.at[base + n], nss.at[base + n], nsr.at[base + n], dev)
            for n, dev in enumerate(devs)
        ]
        if step == 1:
            for i in range(2, nt - 1):
                gather_third(i)
                upstream(i)
        for n, copy in enumerate(batch):
            copy.wait_recv()
            v = v + nrecv[base + n]
        base += len(devs)
    total_square = jnp.sum(jnp.sum(v, axis=1, keepdims=True), axis=0, keepdims=True)
    limit = math.sqrt(kbt.shape[0] * width)
    clip = jnp.minimum(1.0, limit / (jnp.sqrt(total_square) + 1e-06))
    nat = pl.multiple_of(c * rows, rows)

    @pl.loop(0, rows // 16)
    def _(g):
        r = pl.ds(pl.multiple_of(g * 16, 16), 16)
        clipped = gsum[r, :] * clip
        first = beta_one * m1[r, :] + (1.0 - beta_one) * clipped
        second = beta_two * m2[r, :] + (1.0 - beta_two) * clipped * clipped
        nf[r, :] = first
        ns[r, :] = second
        nwb[q, pl.ds(pl.multiple_of(nat + g * 16, 16), 16), :] = (
            w[r, :].astype(F32) * (1.0 - learn_rate * decay_rate)
            - learn_rate * first / (jnp.sqrt(second) + eps_adam)
        ).astype(BF16)

    def piece_of(yy, xx, part):
        return nwb.at[yy * nqx + xx, pl.ds(nat, rows), part]

    w_first = []
    for k in range(1, nqx):
        part = piece_of(qy, qx, ha)
        w_first.append(remote(part, part, ws.at[k - 1], wr.at[k - 1], dev_x(k)))
    for k in range(1, nqy):
        n = nqx - 1 + k - 1
        part = piece_of(qy, qx, hb)
        w_first.append(remote(part, part, ws.at[n], wr.at[n], dev_y(k)))

    gather_third(nt - 1)
    upstream(nt - 1)

    for copy in w_first:
        copy.wait_recv()
    w_second = []
    for k in range(1, nqy):
        for xx in range(nqx):
            part = piece_of(qy, xx, ha)
            n = len(w_second)
            w_second.append(remote(part, part, vs.at[n], vr.at[n], dev_y(k)))
    for k in range(1, nqx):
        for yy in range(nqy):
            part = piece_of(yy, qx, hb)
            n = len(w_second)
            w_second.append(remote(part, part, vs.at[n], vr.at[n], dev_x(k)))

    outs = []
    for k in range(ntile):
        piece = pl.ds(k * tile, tile)

        @pl.loop(0, tile // 16)
        def _(g):
            r = pl.ds(pl.multiple_of(k * tile + g * 16, 16), 16)
            s = sinv[r, :1]
            inner = s * (jnp.sum(cross[r, :], axis=1, keepdims=True) / width)
            normed[r, :] = (
                s * (normed[r, :].astype(F32) - x[r, :].astype(F32) * s * inner)
            ).astype(BF16)

        copy = pltpu.make_async_copy(normed.at[piece], ig_hbm.at[piece], osem.at[k])
        copy.start()
        outs.append(copy)

    for copy in w_second:
        copy.wait_recv()
    part = nwb.at[:, pl.ds(nat, rows)]
    last = remote(part, part, vs.at[nb], vr.at[nb], (mate, t))
    last.wait_recv()
    copy = pltpu.make_async_copy(nwb, nw_hbm, lsem)
    copy.start()
    for copy_out in outs:
        copy_out.wait()
    for sent in sends:
        sent.wait_send()
    copy.wait()


def body(ndp, nt, norm_input, key_grad, positions, norm_gain, key_weight, first_moment, second_moment):
    rows, cols = key_weight.shape
    tokens, width = norm_input.shape
    nq = ndp // 2
    features = ndp * rows
    back = unrotate(key_grad, positions)
    back = back.reshape(tokens, nq, 2, rows).transpose(0, 2, 1, 3).reshape(tokens, features)
    tile = min(128, tokens)
    ntile = tokens // tile
    any_spec = pl.BlockSpec(memory_space=pl.ANY)
    vmem = pl.BlockSpec(memory_space=pltpu.VMEM)
    dma = pltpu.SemaphoreType.DMA
    nqx = math.isqrt(nq)
    while nq % nqx:
        nqx -= 1
    nqy = nq // nqx
    hc = cols // 2
    na = nqx + nqy - 2
    nb = (nqx - 1) * nqy + (nqy - 1) * nqx
    nn = 1 + na + nt - 1
    scratch = [
        pltpu.VMEM((tokens, width), BF16),
        pltpu.VMEM((tokens, width), BF16),
        pltpu.VMEM((nt, features, cols), BF16),
        pltpu.VMEM((nt, features, cols), BF16),
        pltpu.VMEM((nt, nq * rows, cols), BF16),
        pltpu.VMEM((nt, (nqx - 1) * nqy, rows, hc), BF16),
        pltpu.VMEM((nt, (nqy - 1) * nqx, rows, hc), BF16),
        pltpu.VMEM((nt, nqy - 1, rows, hc), BF16),
        pltpu.VMEM((nt, nqx - 1, rows, hc), BF16),
        pltpu.VMEM((nt - 1, rows, cols), BF16),
        pltpu.VMEM((nt - 1, rows, cols), BF16),
        pltpu.VMEM((rows, cols), F32),
        pltpu.VMEM((tokens, 128), F32),
        pltpu.VMEM((tokens, 128), F32),
        pltpu.VMEM((nq, 2 * rows, cols), BF16),
        pltpu.VMEM((4, 8, 128), F32),
        pltpu.VMEM((nn, 8, 128), F32),
        dma, dma((ntile,)), dma((ntile,)),
    ]
    for count in (nt - 1, nt * na, nt, nt * nb, nt, nt * nb, nt * na, nt - 1, nn, na, nb + 1):
        scratch += [dma((count,)), dma((count,))]
    input_grad, new_weight, new_first, new_second = pl.pallas_call(
        functools.partial(kernel, ndp, nt, nqx),
        out_shape=(
            jax.ShapeDtypeStruct((tokens, width), BF16),
            jax.ShapeDtypeStruct((nq, 2 * rows, cols), BF16),
            jax.ShapeDtypeStruct((rows, cols), F32),
            jax.ShapeDtypeStruct((rows, cols), F32),
        ),
        in_specs=[any_spec] + [vmem] * 6,
        out_specs=(any_spec, any_spec, vmem, vmem),
        scratch_shapes=scratch,
        compiler_params=pltpu.CompilerParams(
            collective_id=0, has_side_effects=True, vmem_limit_bytes=62 * 2**20
        ),
    )(
        norm_input, back, back.T, norm_gain.astype(F32)[None, :], key_weight, first_moment, second_moment,
    )
    return (input_grad, new_weight.reshape(features, cols), new_first, new_second)


def solution(mesh):
    in_specs = (
        P(("dp", "tensor"), None),
        P(("dp", "tensor"), None),
        P(("dp", "tensor")),
        P(),
        P("dp", "tensor"),
        P("dp", "tensor"),
        P("dp", "tensor"),
    )
    out_specs = (P(("dp", "tensor"), None), P(None, "tensor"), P("dp", "tensor"), P("dp", "tensor"))
    return jax.shard_map(
        functools.partial(body, mesh.shape["dp"], mesh.shape["tensor"]),
        mesh=mesh, in_specs=in_specs, out_specs=out_specs, check_vma=False,
    )
```
